32 devices in a mesh: gx: 16 (over z, y, x), gz: 2 (over core).
Axes of the slice: x: 2, y: 2, z: 4, core: 2. Of those that a mesh axis runs over, the one named last changes fastest.
Arguments:
- modes: bfloat16 [2, 192, 96, 3, 128], P(None, 'gx', 'gz'), may hold values from -6 to 6
- wall_grad: bfloat16 [2, 192, 96, 3, 128], P(None, 'gx', 'gz'), may hold values from -6 to 6
Outputs:
- convective: float32 [128, 128, 128], P('gx', 'gz')
The draws below stay inside these ranges and needn't reach their ends.
All inputs are finite; a program needn't handle non-finite values.
Results may differ from the reference program's by a relative error of at most 0.0038.
Values may be sent and summed in bfloat16 or wider, within the bound.
No kernel may reach another device: no remote copies, remote signals or barrier semaphores. Data moves between devices by JAX's collectives and lax.ppermute only.
A program may use at most 64 MiB of HBM per device.

```python
import math
import jax
import jax.numpy as jnp
from jax import lax

M = 128
PLANES = 2
NX = 192
NZ = 96


def block_scale(key, dims, shards, least, high):
    gain, own = 1.0, jax.random.fold_in(key, 6)
    for position, parts in shards:
        steps = jnp.exp(jax.random.uniform(jax.random.fold_in(own, position), (parts,), jnp.float32, least / len(shards), high / len(shards)))
        gain = gain * jnp.repeat(steps, dims[position] // parts).reshape([-1 if axis == position else 1 for axis in range(len(dims))])
    return gain


def normal_values(rng, dims, scale, reach, split=(), held_as=jnp.bfloat16):
    values = scale * jax.random.normal(rng, dims, jnp.float32)
    if split:
        values = values * block_scale(rng, dims, split, -0.22, 0.18)
    return jnp.clip(values, -reach, reach).astype(held_as)


def setup_inputs(seed: int = 0) -> dict:
    seeds = jax.random.split(jax.random.key(seed), 3)
    return {
        "modes": normal_values(seeds[0], (PLANES, NX, NZ, 3, M), 1.0, 6.0, ((1, 16), (2, 2))),
        "wall_grad": normal_values(seeds[1], (PLANES, NX, NZ, 3, M), 1.0, 6.0, ((1, 16), (2, 2))),
    }


def derive(field, axis):
    coefs = (0.75, -0.15, 1.0 / 60.0)
    total = jnp.zeros_like(field)
    for shift_by, coef in zip((1, 2, 3), coefs):
        total = total + coef * (jnp.roll(field, -shift_by, axis) - jnp.roll(field, shift_by, axis))
    return total

def reference(modes, wall_grad):
    weight = 1.0 / math.sqrt(PLANES * NX * NZ)
    result = jnp.zeros((M, M, M), jnp.float32)
    block = 4
    for plane in range(PLANES):
        phi = modes[plane]
        field = phi.astype(jnp.float32)
        grad_x = derive(field, 0).astype(jnp.bfloat16).reshape(-1, 3, M)
        grad_z = derive(field, 1).astype(jnp.bfloat16).reshape(-1, 3, M)
        grad_y = wall_grad[plane].reshape(-1, 3, M)
        flat = phi.reshape(-1, 3, M)
        points = flat.shape[0]
        left = flat.reshape(points * 3, M)

        def one_block(index):
            start = (index * block).astype(jnp.int32)
            adv = jnp.zeros((points, 3, block, M), jnp.float32)
            for comp, grad in enumerate((grad_x, grad_y, grad_z)):
                part = lax.dynamic_slice_in_dim(grad, start, block, 2).astype(jnp.float32)
                adv = adv + part[:, :, :, None] * flat[:, comp, None, None, :].astype(jnp.float32)
            adv = adv.astype(jnp.bfloat16).reshape(points * 3, block * M)
            prod = lax.dot_general(left, adv, (((0,), (0,)), ((), ())), preferred_element_type=jnp.float32)
            return jnp.transpose(prod.reshape(M, block, M), (1, 0, 2))
        blocks = lax.map(one_block, jnp.arange(M // block, dtype=jnp.int32))
        result = result + blocks.reshape(M, M, M)
    return result * weight
```

```python
import functools
import math

import jax
import jax.numpy as jnp
from jax import lax
from jax.experimental import pallas as pl
from jax.experimental.pallas import tpu as pltpu
from jax.sharding import PartitionSpec as P

HALO = 3
TILE = 256
WIDE = 128
MODES_OF = ("b", "b", "f")
COEFS = (0.75, -0.15, 1.0 / 60.0)


def ring(count, step):
    return [(i, (i + step) % count) for i in range(count)]


def prep_kernel(xs, planes, zs, gran, scal_ref, m_ref, w_ref, gb_ref, gf_ref, mt_ref, wn_ref, tmp_ref):
    t = pl.program_id(0)
    xor = scal_ref[0]
    row0 = pl.multiple_of(scal_ref[1], 8)
    rows = planes * zs
    comps, _, modes = wn_ref.shape[1:]
    modes //= 2
    keep = mt_ref.shape[2]
    gx, gy, gz, own = [], [], [], []
    for xi in range(xs):
        base = t * xs + xi + HALO
        mid = m_ref[base]
        total = jnp.zeros(mid.shape, jnp.float32)
        for shift, coef in zip((1, 2, 3), COEFS):
            upper = m_ref[base + shift].astype(jnp.float32)
            lower = m_ref[base - shift].astype(jnp.float32)
            total = total + coef * (upper - lower)
        gx.append(total)
        f = mid.astype(jnp.float32)
        parts = []
        for plane in range(planes):
            g = f[plane * zs : (plane + 1) * zs]
            total = jnp.zeros(g.shape, jnp.float32)
            for shift, coef in zip((1, 2, 3), COEFS):
                total = total + coef * (pltpu.roll(g, zs - shift, 0) - pltpu.roll(g, shift, 0))
            parts.append(total)
        gz.append(jnp.concatenate(parts, 0))
        gy.append(w_ref[t * xs + xi].astype(jnp.float32))
        own.append(f)
    grads = [jnp.concatenate(g, 0) for g in (gx, gy, gz)]
    flat = jnp.concatenate(own, 0)
    zero = jnp.zeros((xs * rows, modes), jnp.bfloat16)
    ib = jf = 0
    for c in range(comps):
        cols = slice(c * modes, (c + 1) * modes)
        wn_ref[0, c, :, 0:modes] = flat[:, cols].astype(jnp.bfloat16)
        wn_ref[0, c, :, modes : 2 * modes] = zero
        tmp_ref[...] = flat[:, cols].T
        mt_ref[0, c] = tmp_ref[pl.ds(row0, keep), :]
        for a in range(3):
            g = grads[a][:, cols].astype(jnp.bfloat16).astype(jnp.float32)
            tmp_ref[...] = g.T
            for b in range(modes // gran):
                src = pl.multiple_of((b ^ xor) * gran, 8)
                v = tmp_ref[pl.ds(src, gran), :]
                if MODES_OF[c] == "b":
                    gb_ref[0, ib, b * gran : (b + 1) * gran, :] = v.astype(jnp.bfloat16)
                else:
                    gf_ref[0, jf, b * gran : (b + 1) * gran, :] = v
            if MODES_OF[c] == "b":
                ib += 1
            else:
                jf += 1


def prepare(mfull, wfull, xor, row0, keep, modes, gran):
    cells, planes, zs, comps_modes = wfull.shape
    comps = comps_modes // modes
    rows = planes * zs
    xs = WIDE // math.gcd(rows, WIDE)
    points = cells * rows
    step = xs * rows
    wide = TILE * math.gcd(points // TILE, 9)
    chunks, steps = points // wide, wide // step
    nb, nf = MODES_OF.count("b"), MODES_OF.count("f")
    scal = jnp.stack([xor, row0]).astype(jnp.int32)
    return pl.pallas_call(
        functools.partial(prep_kernel, xs, planes, zs, gran),
        grid_spec=pltpu.PrefetchScalarGridSpec(
            num_scalar_prefetch=1,
            grid=(cells // xs,),
            in_specs=[
                pl.BlockSpec((cells + 2 * HALO, rows, comps_modes), lambda t, s: (0, 0, 0), pipeline_mode=pl.Buffered(1)),
                pl.BlockSpec((cells, rows, comps_modes), lambda t, s: (0, 0, 0), pipeline_mode=pl.Buffered(1)),
            ],
            out_specs=[
                pl.BlockSpec((1, 3 * nb, modes, step), lambda t, s: (t // steps, 0, 0, t % steps)),
                pl.BlockSpec((1, 3 * nf, modes, step), lambda t, s: (t // steps, 0, 0, t % steps)),
                pl.BlockSpec((1, comps, keep, step), lambda t, s: (t // steps, 0, 0, t % steps)),
                pl.BlockSpec((1, comps, step, 2 * modes), lambda t, s: (t // steps, 0, t % steps, 0)),
            ],
            scratch_shapes=[pltpu.VMEM((modes, step), jnp.float32)],
        ),
        out_shape=[
            jax.ShapeDtypeStruct((chunks, 3 * nb, modes, wide), jnp.bfloat16),
            jax.ShapeDtypeStruct((chunks, 3 * nf, modes, wide), jnp.float32),
            jax.ShapeDtypeStruct((chunks, comps, keep, wide), jnp.float32),
            jax.ShapeDtypeStruct((chunks, comps, wide, 2 * modes), jnp.bfloat16),
        ],
        compiler_params=pltpu.CompilerParams(vmem_limit_bytes=28 << 20),
        name="prep",
    )(scal, mfull.reshape(cells + 2 * HALO, rows, comps_modes), wfull.reshape(cells, rows, comps_modes))


def tensor_kernel(jobs, gran, gb_ref, gf_ref, mt_ref, wn_ref, *outs):
    chunks, _, _, wide = mt_ref.shape
    modes = wn_ref.shape[3] // 2
    for (j_from, j_count, blocks), o_ref in zip(jobs, outs):
        rows = len(blocks) * gran
        per = min(TILE // rows if rows < TILE else 1, j_count // 2)
        group = 2 * per

        def step(t, _, j_from=j_from, blocks=blocks, o_ref=o_ref, rows=rows, per=per, group=group):
            j0 = j_from + t * group

            def scoped(*accs):
                def tiles(n):
                    stage = 0
                    for pt in range(wide // TILE):
                        cols = pl.ds(pt * TILE, TILE)
                        ib = jf = 0
                        for c, kind in enumerate(MODES_OF):
                            w = wn_ref[n, c, cols, :]
                            for x in range(2):
                                pltpu.matmul_push_rhs(w, stage, x)
                            for q in range(per):
                                ms = []
                                for x in range(2):
                                    j = j0 + x * per + q
                                    m = [jnp.broadcast_to(mt_ref[n, a, pl.ds(j, 1), cols], (8, TILE)) for a in range(3)]
                                    if kind == "b":
                                        m = [v.astype(jnp.bfloat16) for v in m]
                                    ms.append(m)
                                vals = ([], [])
                                for b in blocks:
                                    for h in range(gran // 8):
                                        ks = pl.ds(b * gran + h * 8, 8)
                                        if kind == "b":
                                            g = [gb_ref[n, ib + a, ks, cols] for a in range(3)]
                                        else:
                                            g = [gf_ref[n, jf + a, ks, cols] for a in range(3)]
                                        for x in range(2):
                                            m = ms[x]
                                            vals[x].append(m[0] * g[0] + m[1] * g[1] + m[2] * g[2])
                                for x in range(2):
                                    lhs = jnp.concatenate(vals[x], 0).astype(jnp.bfloat16)
                                    pltpu.matmul_acc_lhs(
                                        accs[x * per + q], lhs, load_staged_rhs=stage if q == 0 else None
                                    )
                            stage ^= 1
                            if kind == "b":
                                ib += 3
                            else:
                                jf += 3

                if chunks == 1:
                    tiles(0)
                else:
                    lax.fori_loop(0, chunks, lambda n, _: (tiles(n), 0)[1], 0)
                for x in range(2):
                    for q in range(per):
                        full = pltpu.matmul_pop(accs[x * per + q])
                        o_ref[t * group + x * per + q] = full[:, :modes].astype(o_ref.dtype)

            pl.run_scoped(scoped, *[pltpu.ACC(x)((rows, TILE), jnp.float32) for x in range(2) for _ in range(per)])
            return 0

        lax.fori_loop(0, j_count // group, step, 0)


def tensor(jobs, gran, dtype, gb, gf, mt, wn, name):
    modes = wn.shape[3] // 2
    rows = sum(j_count * len(blocks) * gran for _, j_count, blocks in jobs)
    return pl.pallas_call(
        functools.partial(tensor_kernel, jobs, gran),
        in_specs=[pl.BlockSpec(memory_space=pltpu.VMEM)] * 4,
        out_specs=[pl.BlockSpec(memory_space=pltpu.VMEM)] * len(jobs),
        out_shape=[
            jax.ShapeDtypeStruct((j_count, len(blocks) * gran, modes), dtype) for _, j_count, blocks in jobs
        ],
        compiler_params=pltpu.CompilerParams(vmem_limit_bytes=24 << 20),
        cost_estimate=pl.CostEstimate(
            flops=2 * rows * mt.shape[1] * mt.shape[0] * mt.shape[3] * modes, bytes_accessed=16 << 20, transcendentals=0
        ),
        name=name,
    )(gb, gf, mt, wn)


def ordered(bits):
    if not bits:
        return [0]
    rest = ordered(bits[1:])
    return [b | bits[0] for b in rest] + rest


def per_device(modes, wall_grad):
    planes, cells_x, cells_z, comps, m = modes.shape
    count_x, count_z = lax.axis_size("gx"), lax.axis_size("gz")
    weight = 1.0 / math.sqrt(planes * cells_x * cells_z * count_x * count_z)
    me, mez = lax.axis_index("gx"), lax.axis_index("gz")
    own = jnp.transpose(modes.reshape(planes, cells_x, cells_z, comps * m), (1, 0, 2, 3))
    wall = jnp.transpose(wall_grad.reshape(planes, cells_x, cells_z, comps * m), (1, 0, 2, 3))
    low = lax.ppermute(own[cells_x - HALO :], "gx", ring(count_x, 1))
    high = lax.ppermute(own[:HALO], "gx", ring(count_x, -1))

    def around(block):
        return [block] + [lax.ppermute(block, "gz", ring(count_z, -s)) for s in range(1, count_z)]

    both = around(jnp.concatenate([own, wall], 0))
    halos = around(jnp.concatenate([low, high], 0))
    mfull = jnp.concatenate(
        [
            jnp.concatenate([h[:HALO] for h in halos], 2),
            jnp.concatenate([b[:cells_x] for b in both], 2),
            jnp.concatenate([h[HALO:] for h in halos], 2),
        ],
        0,
    )
    wfull = jnp.concatenate([b[cells_x:] for b in both], 2)

    slab = m // count_x
    gran = max(8, slab)
    inner = gran // slab
    keep = m // count_z
    operands = prepare(mfull, wfull, me // inner, mez * keep, keep, m, gran)

    bits = [1 << s for s in range((m // gran).bit_length() - 1)]
    order = ordered(bits)
    half = len(order) // 2
    quarter = half // 2
    pieces = (order[:half], order[half : half + quarter], order[half + quarter :])

    def swap(block, bit):
        return lax.ppermute(block.astype(jnp.bfloat16), "gx", [(i, i ^ bit) for i in range(count_x)])

    (first,) = tensor([(0, keep, pieces[0])], gran, jnp.bfloat16, *operands, "first")
    got = swap(first, bits[0] * inner)
    (second,) = tensor([(0, keep, pieces[1])], gran, jnp.float32, *operands, "second")
    (third,) = tensor([(0, keep, pieces[2])], gran, jnp.float32, *operands, "third")
    cut = quarter * gran
    got2 = swap(second + got[:, :cut].astype(jnp.float32), bits[1] * inner)
    rest = third + got[:, cut:].astype(jnp.float32) + got2.astype(jnp.float32)
    for bit in bits[2:]:
        cut = rest.shape[1] // 2
        got = swap(rest[:, :cut], bit * inner)
        rest = rest[:, cut:] + got.astype(jnp.float32)
    bit = inner // 2
    while bit:
        cut = rest.shape[1] // 2
        upper = (me & bit) != 0
        send = jnp.where(upper, rest[:, :cut], rest[:, cut:])
        stay = jnp.where(upper, rest[:, cut:], rest[:, :cut])
        rest = stay + swap(send, bit).astype(jnp.float32)
        bit //= 2
    turned = jnp.transpose(rest, (1, 2, 0)) * weight
    return lax.all_to_all(turned, "gz", 1, 2, tiled=True)


def solution(mesh):
    placed = (P(None, "gx", "gz", None, None), P(None, "gx", "gz", None, None))
    return jax.shard_map(
        per_device, mesh=mesh, in_specs=placed, out_specs=P("gx", "gz", None), check_vma=False
    )
```
